256 devices in a mesh: ctx: 32 (over z, x), rep: 8 (over y, core).
Axes of the slice: x: 4, y: 4, z: 8, core: 2. Of those that a mesh axis runs over, the one named last changes fastest.
Arguments:
- query: bfloat16 [32768, 2048], P(('rep', 'ctx')), parts along dimension 0, may hold values from -6 to 6
- key: bfloat16 [32768, 2048], P(('rep', 'ctx')), parts along dimension 0, may hold values from -6 to 6
- value: bfloat16 [32768, 2048], P(('rep', 'ctx')), parts along dimension 0, may hold values from -6 to 6
- beta: float32 [32768, 16], P(('rep', 'ctx')), parts along dimension 0, may hold values from 0.05 to 0.95
- log_gate: float32 [32768, 16], P(('rep', 'ctx')), parts along dimension 0, may hold values from -1.5 to 0
- level_weight: float32 [32768, 16, 6], P(('rep', 'ctx')), parts along dimension 0, may hold values from 0.1 to 1.5
- norm_gain: float32 [128], replicated, may hold values from 0.5 to 1.5
- grad_out: bfloat16 [32768, 2048], P(('rep', 'ctx')), parts along dimension 0, may hold values from -6 to 6
- grad_final_state: float32 [16384, 128], P(('rep', 'ctx')), parts along dimension 0, may hold values from -6 to 6
Outputs:
- grad_query: bfloat16 [32768, 2048], P(('rep', 'ctx')), parts along dimension 0
- grad_key: bfloat16 [32768, 2048], P(('rep', 'ctx')), parts along dimension 0
- grad_value: bfloat16 [32768, 2048], P(('rep', 'ctx')), parts along dimension 0
- grad_beta: float32 [32768, 16], P(('rep', 'ctx')), parts along dimension 0
- grad_level: float32 [32768, 16, 6], P(('rep', 'ctx')), parts along dimension 0
- grad_gain: float32 [1024], P('rep'), parts along dimension 0
- final_state: float32 [16384, 128], P(('rep', 'ctx')), parts along dimension 0
The draws below stay inside these ranges and needn't reach their ends.
There are 8 independent parts, one for each index of `rep`. The reference program is written for one: setup_inputs(seed, part) draws one part's arguments, and reference() takes and returns one part's arrays. A program takes and returns all parts, laid end to end along the dimension named above; an argument that names none is the same for every part. Nothing has to cross between parts.
All inputs are finite; a program needn't handle non-finite values.
Results may differ from the reference program's by a relative error of at most 0.001.
Values sent between devices are 32-bit elements; how exact they have to be, the bound alone decides.
No kernel may reach another device: no remote copies, remote signals or barrier semaphores. Data moves between devices by JAX's collectives and lax.ppermute only.
A program may use at most 128 MiB of HBM per device.

```python
import jax
import jax.numpy as jnp
from jax import lax

HEAD_TOTAL = 16
DK = 128
DV = 128
TOK_DEV = 128
SEQUENCE_TOKENS = 4096
LEVELS = 6
N_CTX = 32


def draw_log_gate(key, part):
    base_key = jax.random.fold_in(key, 11)
    key_sequence = jax.random.split(base_key, 7)
    fast_share = 0.5
    is_fast = jax.random.uniform(key_sequence[0], (HEAD_TOTAL,)) < fast_share
    fast_rate = 1.0 / jax.random.uniform(key_sequence[1], (HEAD_TOTAL,), minval=30.0, maxval=50.0)
    slow_rate = jnp.exp(jax.random.uniform(key_sequence[2], (HEAD_TOTAL,), minval=jnp.log(0.05), maxval=jnp.log(0.3))) / SEQUENCE_TOKENS
    head_rates = jnp.where(is_fast, fast_rate, slow_rate)
    block_factor = jnp.exp(jax.random.uniform(key_sequence[3], (SEQUENCE_TOKENS // TOK_DEV, HEAD_TOTAL), minval=-0.7, maxval=0.7))
    block_factor = jnp.repeat(block_factor, TOK_DEV, axis=0)
    token_factor = jax.random.uniform(key_sequence[4], (SEQUENCE_TOKENS, HEAD_TOTAL), minval=0.5, maxval=1.5)
    gate_logarithms = -head_rates[None, :] * block_factor * token_factor
    flush_position = jax.random.randint(key_sequence[5], (2, HEAD_TOTAL), 0, SEQUENCE_TOKENS)
    flush_keep_mask = jax.random.uniform(key_sequence[6], (2, HEAD_TOTAL), minval=0.5, maxval=0.8)
    token_positions = jnp.arange(SEQUENCE_TOKENS, dtype=jnp.int32)
    match_mask = token_positions[None, :, None] == flush_position[:, None, :]
    gate_logarithms = gate_logarithms + jnp.sum(jnp.where(match_mask, jnp.log(flush_keep_mask)[:, None, :], 0.0), axis=0)
    return gate_logarithms.astype(jnp.float32)


def draw_key(key, part):
    base_key = jax.random.fold_in(key, 23)
    key_sequence = jax.random.split(base_key, 3)
    block_count = SEQUENCE_TOKENS // TOK_DEV
    pair_count = block_count * HEAD_TOTAL
    ranking = jax.random.permutation(key_sequence[0], pair_count)
    aligned = (ranking < pair_count // 2).reshape(block_count, 1, HEAD_TOTAL, 1)
    direction = jax.random.normal(key_sequence[1], (block_count, 1, HEAD_TOTAL, DK), dtype=jnp.float32)
    noise = jax.random.normal(key_sequence[2], (block_count, TOK_DEV, HEAD_TOTAL, DK), dtype=jnp.float32)
    strength = 2.5
    entries = noise + jnp.where(aligned, strength * direction, 0.0)
    entries = jnp.clip(entries, -6.0, 6.0)
    return entries.reshape(SEQUENCE_TOKENS, HEAD_TOTAL * DK).astype(jnp.bfloat16)


def level_of(stream_key, dims, pieces, smallest, top_value):
    level = 1.0
    for position, parts in pieces:
        steps = jax.random.uniform(jax.random.fold_in(jax.random.fold_in(stream_key, 6), position), (parts,), jnp.float32, smallest / len(pieces), top_value / len(pieces))
        level = level * jnp.repeat(jnp.exp(steps), dims[position] // parts).reshape((-1,) + (1,) * (len(dims) - 1 - position))
    return level


def bell_draw(stream_key, shape, spread, most, cuts=(), kind=jnp.bfloat16):
    result = spread * jax.random.normal(stream_key, shape, jnp.float32)
    if cuts:
        result = result * level_of(stream_key, shape, cuts, -0.22, 0.18)
    return jnp.clip(result, -most, most).astype(kind)


def setup_inputs(seed: int = 0, part: int = 0) -> dict:
    keys = jax.random.split(jax.random.key(seed), 10)
    part_keys = jax.random.split(jax.random.fold_in(keys[9], part), 10)
    query = bell_draw(part_keys[0], (SEQUENCE_TOKENS, HEAD_TOTAL * DK), 1.0, 6.0, ((0, 32),))
    key = draw_key(jax.random.fold_in(jax.random.fold_in(keys[9], part), 71), part)
    value = bell_draw(part_keys[2], (SEQUENCE_TOKENS, HEAD_TOTAL * DV), 1.0, 6.0, ((0, 32),))
    beta = jnp.clip(0.05 + 0.9 * jax.random.uniform(part_keys[3], (SEQUENCE_TOKENS, HEAD_TOTAL), jnp.float32) ** level_of(part_keys[3], (SEQUENCE_TOKENS, HEAD_TOTAL), ((0, 32),), -0.2, 0.2), 0.05, 0.95)
    log_gate = draw_log_gate(jax.random.fold_in(jax.random.fold_in(keys[9], part), 71), part)
    level_weight = jnp.clip(0.1 + 1.4 * jax.random.uniform(part_keys[5], (SEQUENCE_TOKENS, HEAD_TOTAL, LEVELS), jnp.float32) ** level_of(part_keys[5], (SEQUENCE_TOKENS, HEAD_TOTAL, LEVELS), ((0, 32),), -0.2, 0.2), 0.1, 1.5)
    norm_gain = jnp.clip(1.0 + 0.1 * jax.random.normal(keys[6], (DV,), jnp.float32), 0.5, 1.5)
    grad_out = bell_draw(part_keys[7], (SEQUENCE_TOKENS, HEAD_TOTAL * DV), 1.0, 6.0, ((0, 32),))
    grad_final_state = bell_draw(part_keys[8], (HEAD_TOTAL * DK, DV), 1.0, 6.0, ((0, 32),), jnp.float32)
    return dict(query=query, key=key, value=value, beta=beta, log_gate=log_gate, level_weight=level_weight, norm_gain=norm_gain, grad_out=grad_out, grad_final_state=grad_final_state)


epsilon = 1e-06
topmost_level = lax.Precision.HIGHEST

def normalize(values):
    return values * lax.rsqrt(lax.optimization_barrier(jnp.sum(values * values, axis=-1, keepdims=True)) + epsilon)

def split_heads(values, head_count):
    row_count = values.shape[0]
    return values.reshape(row_count, head_count, -1).transpose(1, 0, 2)

def prepare(query, key, value, beta, cum_gate):
    head_count = cum_gate.shape[0]
    row_count = cum_gate.shape[1]
    query_normed = normalize(split_heads(query, head_count))
    normalized_key = normalize(split_heads(key, head_count))
    value_heads = split_heads(value, head_count)
    beta_heads = beta.T
    strict = jnp.tril(jnp.ones((row_count, row_count), dtype=bool), -1)
    log_gaps = cum_gate[:, :, None] - cum_gate[:, None, :]
    decays = jnp.exp(jnp.where(strict[None], log_gaps, -jnp.inf))
    key_inner = jnp.einsum('htk,hsk->hts', normalized_key, normalized_key, precision=topmost_level)
    system = jnp.eye(row_count, dtype=cum_gate.dtype)[None] + beta_heads[:, :, None] * decays * key_inner
    surrogate_value = jax.scipy.linalg.solve_triangular(system, beta_heads[:, :, None] * value_heads, lower=True)
    trailing_decay = jnp.exp(cum_gate[:, -1:] - cum_gate)
    state_per_block = jnp.einsum('fni,fnb->fib', normalized_key * trailing_decay[:, :, None], surrogate_value, precision=topmost_level)
    return (query_normed, normalized_key, surrogate_value, state_per_block)

def finish(query_normed, normalized_key, surrogate_value, level_weight, norm_gain, bucket_states, cum_gate):
    row_count = cum_gate.shape[1]
    inclusive = jnp.tril(jnp.ones((row_count, row_count), dtype=bool))
    log_gaps = cum_gate[:, :, None] - cum_gate[:, None, :]
    decays = jnp.exp(jnp.where(inclusive[None], log_gaps, -jnp.inf))
    attention_scores = jnp.einsum('htk,hsk->hts', query_normed, normalized_key, precision=topmost_level) * decays
    intra_out = jnp.einsum('hts,hsv->htv', attention_scores, surrogate_value, precision=topmost_level)
    cross_out = jnp.einsum('htk,lhkv->lhtv', query_normed, bucket_states, precision=topmost_level)
    level_heads = level_weight.transpose(1, 0, 2)
    weighted = level_heads[:, :, 1:] * jnp.exp(cum_gate)[:, :, None]
    mixture = level_heads[:, :, 0:1] * intra_out + jnp.einsum('htl,lhtv->htv', weighted, cross_out, precision=topmost_level)
    inverse_rms = lax.rsqrt(lax.optimization_barrier(jnp.mean(mixture * mixture, axis=-1, keepdims=True)) + epsilon)
    normed = mixture * inverse_rms * norm_gain
    return normed.transpose(1, 0, 2).reshape(row_count, -1)

def reference(query, key, value, beta, log_gate, level_weight, norm_gain, grad_out, grad_final_state):
    blocks = N_CTX
    row_count = TOK_DEV
    cum_gates = jnp.cumsum(log_gate.reshape(blocks, row_count, HEAD_TOTAL).transpose(0, 2, 1), axis=2)
    totals = cum_gates[:, :, -1]
    block_ends = jnp.cumsum(totals, axis=0)
    starts = block_ends - totals
    closing_coefficients = jnp.exp(block_ends[-1:, :] - block_ends)
    block_ids = jnp.arange(blocks, dtype=jnp.int32)
    xor_ids = jnp.bitwise_xor(block_ids[:, None], block_ids[None, :])
    earlier = block_ids[None, :] < block_ids[:, None]
    gaps = jnp.where(earlier[:, :, None], starts[:, None, :] - block_ends[None, :, :], -jnp.inf)
    coeffs = jnp.exp(gaps)
    level_spans = 2 ** jnp.arange(LEVELS - 1, dtype=jnp.int32)
    member = (xor_ids[:, None, :] >= level_spans[None, :, None]) & (xor_ids[:, None, :] < 2 * level_spans[None, :, None])
    weights = member[:, :, :, None].astype(totals.dtype) * coeffs[:, None, :, :]

    def forward(query_float, key_float, value_float, beta_float, level_float, gain_float):
        inputs = (query_float.reshape(blocks, row_count, -1), key_float.reshape(blocks, row_count, -1), value_float.reshape(blocks, row_count, -1), beta_float.reshape(blocks, row_count, HEAD_TOTAL), cum_gates)
        query_normed, normalized_key, surrogate_value, per_block_state_list = lax.map(lambda packed: prepare(*packed), inputs)

        def finish_block(packed):
            query_block, key_block, pseudo_block, level_block, gate_block, weight_block = packed
            bucket_states = jnp.einsum('ljh,jhkv->lhkv', weight_block, per_block_state_list, precision=topmost_level)
            return finish(query_block, key_block, pseudo_block, level_block, gain_float, bucket_states, gate_block)
        results = lax.map(finish_block, (query_normed, normalized_key, surrogate_value, level_float.reshape(blocks, row_count, HEAD_TOTAL, LEVELS), cum_gates, weights))
        closing_value = jnp.einsum('re,recy->ecy', closing_coefficients, per_block_state_list, precision=topmost_level)
        return (results.reshape(blocks * row_count, -1), closing_value.reshape(HEAD_TOTAL * DK, DV))
    primals = (query.astype(jnp.float32), key.astype(jnp.float32), value.astype(jnp.float32), beta, level_weight, norm_gain)
    results, backward = jax.vjp(forward, *primals)
    grads = backward((grad_out.astype(jnp.float32), grad_final_state))
    return (grads[0].astype(jnp.bfloat16), grads[1].astype(jnp.bfloat16), grads[2].astype(jnp.bfloat16), grads[3], grads[4], grads[5], results[1])
```

```python
import jax
import jax.numpy as jnp
from jax import lax
from jax.experimental import pallas as pl
from jax.experimental.pallas import tpu as pltpu
from jax.sharding import PartitionSpec as P


EPS = 1e-06
F32 = jnp.float32
BF16 = jnp.bfloat16
N = 128
HALF = 64
GROUP = 4
LEVELS = 5
INTERPRET = False

NN = ((1,), (0,))
NT = ((1,), (1,))
TN = ((0,), (0,))


def dot(a, b, dims):
    return lax.dot_general(a, b, (dims, ((), ())), preferred_element_type=F32)


def split(a):
    hi = a.astype(BF16)
    return hi, (a - hi.astype(F32)).astype(BF16)


def cat(parts, axis):
    return jnp.concatenate(parts, axis=axis)


def dot_left(a, b, dims=NN):
    hi, lo = split(a)
    ca, cb = dims[0][0], dims[1][0]
    return dot(cat([hi, lo], ca), cat([b, b], cb), dims)


def dot_split(a, b, dims=NN):
    ca, cb = dims[0][0], dims[1][0]
    return dot(cat([a[0], a[1]], ca), cat([b[0], b[0]], cb), dims) + dot(a[0], b[1], dims)


def dot_full(a, b, dims=NN):
    return dot_split(split(a), split(b), dims)


def iotas():
    return (
        lax.broadcasted_iota(jnp.int32, (N, N), 0),
        lax.broadcasted_iota(jnp.int32, (N, N), 1),
    )


def inv_norm_col(raw):
    return lax.rsqrt(jnp.sum(raw * raw, axis=1, keepdims=True) + EPS)


def unit_lower_inverse(lowers, mask_ref):
    row16 = lax.broadcasted_iota(jnp.int32, (16, N), 0)
    col16 = lax.broadcasted_iota(jnp.int32, (16, N), 1)
    base = col16 & 112
    start = jnp.where((col16 & 15) == row16, 1.0, 0.0).astype(F32)
    packed = [(a * mask_ref[1]).reshape(8, 16, N).sum(axis=0) for a in lowers]
    inverses = [start for _ in lowers]
    for j in range(15):
        index = base | j
        for h, rows in enumerate(packed):
            column = jnp.take_along_axis(rows, index, axis=1, mode="promise_in_bounds")
            inverses[h] = inverses[h] - column * inverses[h][j : j + 1, :]
    inverses = [jnp.broadcast_to(a[None], (8, 16, N)).reshape(N, N) * mask_ref[1] for a in inverses]
    for level in range(3):
        pairs = [split(a) for a in inverses]
        inner = [dot_split(split(a * mask_ref[2 + level]), p) for a, p in zip(lowers, pairs)]
        inverses = [a - dot_split(p, split(c)) for a, p, c in zip(inverses, pairs, inner)]
    return inverses


def fill_masks(mask_ref):
    row, col = iotas()
    mask_ref[0] = jnp.where(row > col, 0.0, -1e30)
    mask_ref[1] = jnp.where((row >> 4) == (col >> 4), 1.0, 0.0)
    for level in range(3):
        bits = 4 + level
        below = ((row >> bits) & 1 == 1) & ((col >> bits) == (row >> bits) - 1)
        mask_ref[2 + level] = jnp.where(below, 1.0, 0.0)
    mask_ref[5] = jnp.where(row == col, 1.0, 0.0)


def token_sums(gate_ref, beta_ref, cols_ref, rows_ref, total_ref):
    row, col = iotas()
    gate = gate_ref[...]
    beta = beta_ref[...]
    upper = jnp.where(row <= col, 1.0, 0.0).astype(BF16)
    hi, lo = split(gate)
    rest = (gate - hi.astype(F32) - lo.astype(F32)).astype(BF16)
    cum = dot(cat([hi, lo, rest], 1), cat([upper] * 3, 0), NN)
    total_ref[...] = jnp.broadcast_to(cum[:, N - 1 : N], cum.shape)
    columns = cat([cum, beta], 0).T
    for s in range(4):
        part = slice(s * GROUP, (s + 1) * GROUP)
        rows_ref[s] = cat([cum[part], beta[part]], 0)
        cols_ref[s] = cat([columns[:, part], columns[:, 16 + s * GROUP : 16 + (s + 1) * GROUP]], 1)


def solve_kernel(
    x_ref, gate_ref, beta_ref, key_ref, value_ref,
    r0_ref, r1_ref, r2_ref, r3_ref, s0_ref, s1_ref,
    pseudo_ref, inv_ref, norm_ref, cols_ref, rows_ref, total_ref, mask_ref, gather_ref,
):
    ring_refs = r0_ref, r1_ref, r2_ref, r3_ref
    half_refs = s0_ref, s1_ref
    step = pl.program_id(0)
    x = x_ref[0]

    @pl.when(step == 0)
    def _():
        fill_masks(mask_ref)
        token_sums(gate_ref, beta_ref, cols_ref, rows_ref, total_ref)

    cols = cols_ref[step]
    rows = rows_ref[step]

    group = range(GROUP)
    kb = [key_ref[:, j * N : (j + 1) * N] for j in group]
    inner = [dot(k, k, NT) for k in kb]
    lowers, rk_cols = [], []
    for j in group:
        diagonal = inner[j] * mask_ref[5]
        rk_row = lax.rsqrt(jnp.sum(diagonal, axis=0, keepdims=True) + EPS)
        rk_cols.append(lax.rsqrt(jnp.sum(diagonal, axis=1, keepdims=True) + EPS))
        norm_ref[0, j : j + 1, :] = rk_row
        decay = jnp.exp((cols[:, j : j + 1] - rows[j : j + 1]) + mask_ref[0])
        lowers.append((cols[:, GROUP + j : GROUP + j + 1] * rk_cols[j]) * (decay * (rk_row * inner[j])))
    inverses = unit_lower_inverse(lowers, mask_ref)
    for j in group:
        inv_ref[j] = inverses[j]
    pseudos = [
        dot_left(inverses[j] * rows[GROUP + j : GROUP + j + 1], value_ref[:, j * N : (j + 1) * N])
        for j in group
    ]
    states = []
    for j in group:
        pseudo_ref[j] = pseudos[j]
        trailing = jnp.exp(rows[j : j + 1, N - 1 : N] - cols[:, j : j + 1]) * rk_cols[j]
        hi, lo = split(pseudos[j] * trailing)
        states.append(dot(cat([kb[j], kb[j]], 0), cat([hi, lo], 0), TN))
    for j in group:
        for half in range(2):
            rows = slice((j >> 1) * HALF, (j >> 1) * HALF + HALF)
            gather_ref[2 * (j & 1) + half, rows, :] = states[j][half * HALF : (half + 1) * HALF]
    base = pl.multiple_of(step * N, N)
    for slot in range(4):
        part = gather_ref[x ^ slot]
        ring_refs[slot][pl.ds(base, N), :] = part
        half_refs[slot >> 1][slot & 1] = part

    @pl.when(step == pl.num_programs(0) - 1)
    def _():
        for slot in range(4):
            ring_refs[slot][4 * N : 4 * N + 16, :] = total_ref[...]


def intra_kernel(query_ref, key_ref, cols_ref, rows_ref, norm_ref, pseudo_ref, intra_ref):
    row, col = iotas()
    group = range(GROUP)
    qb = [query_ref[:, j * N : (j + 1) * N] for j in group]
    products = [dot(qb[j], key_ref[:, j * N : (j + 1) * N], NT) for j in group]
    penalty = jnp.where(row >= col, 0.0, -1e30)
    scores = []
    for j in group:
        rq_col = inv_norm_col(qb[j].astype(F32))
        decay = jnp.exp((cols_ref[0, :, j : j + 1] - rows_ref[0, j : j + 1, :]) + penalty)
        scores.append(rq_col * (products[j] * norm_ref[0, j : j + 1, :]) * decay)
    for j in group:
        intra_ref[j] = dot_full(scores[j], pseudo_ref[j])


def place_pieces(x, pieces, scratch_ref):
    for level in range(3):
        for m in range(4):
            scratch_ref[level, x ^ m] = pieces[4 * level + m][...]


def from_halves(refs, slot, rows):
    return jnp.where(slot < 2, refs[0][slot & 1, rows, :], refs[1][slot & 1, rows, :])


def bucket_of(x, j, level, near_refs, pair_refs, scratch_ref):
    rows = slice((j >> 1) * HALF, (j >> 1) * HALF + HALF)
    parts = []
    for half in range(2):
        quarter = 2 * (j & 1) + half
        if level == 0:
            parts.append(from_halves(near_refs, (x ^ 1) ^ quarter, rows))
        elif level == 1:
            parts.append(from_halves(pair_refs, (x ^ 3) ^ quarter, rows))
        else:
            parts.append(scratch_ref[level - 2, quarter, rows, :])
    return cat(parts, 0)


def cross_kernel(*refs):
    x_ref, query_ref, out_ref, intra_ref, weight_ref, gain_ref = refs[:6]
    near_refs, pair_refs, pieces = refs[6:8], refs[8:10], refs[10:22]
    g1_ref, g2_refs = refs[22], refs[23:25]
    g34_refs, g5_refs = refs[25:29], refs[29:33]
    dm_ref, level_ref = refs[33:35]
    scratch_ref, gather_ref, gain_sum_ref = refs[35:38]
    step = pl.program_id(0)
    x = x_ref[0]
    group = range(GROUP)
    place_pieces(x, pieces, scratch_ref)
    gain = gain_ref[...]
    lane = lax.broadcasted_iota(jnp.int32, (N, 8 * GROUP), 1)
    gain_sum = jnp.zeros((8, N), F32)
    weights = weight_ref[0].T
    levels = jnp.zeros((N, 8 * GROUP), F32)
    qb = [query_ref[:, j * N : (j + 1) * N] for j in group]
    crosses = []
    for j in group:
        pairs = [split(bucket_of(x, j, level, near_refs, pair_refs, scratch_ref)) for level in range(LEVELS)]
        right = cat([cat([p[0] for p in pairs], 1), cat([p[1] for p in pairs], 1)], 0)
        crosses.append(dot(cat([qb[j], qb[j]], 1), right, NN))
    lefts = []
    for j in group:
        go = out_ref[:, j * N : (j + 1) * N].astype(F32)
        rq_col = inv_norm_col(qb[j].astype(F32))
        scaled_weights = weights * jnp.where(lane < GROUP, 1.0, rq_col)
        columns = [
            jnp.broadcast_to(scaled_weights[:, l * GROUP + j : l * GROUP + j + 1], (N, N)) for l in range(LEVELS + 1)
        ]
        intra = intra_ref[j]
        mixture = columns[0] * intra
        for level in range(LEVELS):
            mixture = mixture + columns[level + 1] * crosses[j][:, level * N : (level + 1) * N]
        inverse_rms = lax.rsqrt(jnp.mean(mixture * mixture, axis=1, keepdims=True) + EPS)
        scaled = mixture * inverse_rms
        gain_sum = gain_sum + (go * scaled).reshape(N // 8, 8, N).sum(axis=0)
        dn = go * gain
        dm = inverse_rms * (dn - scaled * jnp.mean(dn * scaled, axis=1, keepdims=True))
        dm_ref[j] = dm
        levels = jnp.where(lane == j, jnp.sum(dm * intra, axis=1, keepdims=True), levels)
        pairs = []
        for level in range(LEVELS):
            along = jnp.sum(dm * crosses[j][:, level * N : (level + 1) * N], axis=1, keepdims=True) * rq_col
            levels = jnp.where(lane == (level + 1) * GROUP + j, along, levels)
            pairs.append(split(dm * columns[level + 1]))
        lefts.append(cat([cat([p[0] for p in pairs], 1), cat([p[1] for p in pairs], 1)], 0))
    level_ref[0] = levels.T
    for j in group:
        grads = dot(cat([qb[j], qb[j]], 0), lefts[j], TN)
        rows = slice((j >> 1) * HALF, (j >> 1) * HALF + HALF)
        for half in range(2):
            quarter = 2 * (j & 1) + half
            part = grads[half * HALF : (half + 1) * HALF]
            g1_ref[x ^ quarter, rows, :] = part[:, 0:N]
            for level in range(4):
                gather_ref[level, quarter, rows, :] = part[:, (1 + level) * N : (2 + level) * N]
    base = pl.multiple_of(step * N, N)
    for m in range(4):
        g2_refs[m >> 1][m & 1] = gather_ref[0, x ^ m]
        for level in range(2):
            g34_refs[2 * level + (m in (1, 2))][m >> 1] = gather_ref[1 + level, x ^ m]
        g5_refs[m][pl.ds(base, N), :] = gather_ref[3, x ^ m]

    @pl.when(step == 0)
    def _():
        gain_sum_ref[...] = jnp.zeros((8, N), F32)

    gain_sum_ref[...] += gain_sum

    @pl.when(step == pl.num_programs(0) - 1)
    def _():
        for m in range(4):
            g5_refs[m][4 * N : 4 * N + 8, :] = gain_sum_ref[...]


def query_kernel(*refs):
    x_ref, query_ref, key_ref, cols_ref, rows_ref, norm_ref, weight_ref, pseudo_ref, dm_ref = refs[:9]
    near_refs, pair_refs, pieces = refs[9:11], refs[11:13], refs[13:25]
    gq_ref, dp_ref, dk_ref, scratch_ref, mask_ref = refs[25:30]
    x = x_ref[0]
    group = range(GROUP)

    @pl.when(pl.program_id(0) == 0)
    def _():
        row, col = iotas()
        mask_ref[...] = jnp.where(row >= col, 0.0, -1e30)

    place_pieces(x, pieces, scratch_ref)
    qb = [query_ref[:, j * N : (j + 1) * N] for j in group]
    kb = [key_ref[:, j * N : (j + 1) * N] for j in group]
    products = [dot(q, k, NT) for q, k in zip(qb, kb)]
    weights = weight_ref[0].T
    owns = [split(dm_ref[j] * weights[:, j : j + 1]) for j in group]
    dscores = [dot_split(owns[j], split(pseudo_ref[j]), NT) for j in group]
    dqs, rqs = [], []
    for j in group:
        rq_col = inv_norm_col(qb[j].astype(F32))
        rqs.append(rq_col)
        rk_row = norm_ref[0, j : j + 1, :]
        decay = jnp.exp((cols_ref[0, :, j : j + 1] - rows_ref[0, j : j + 1, :]) + mask_ref[...])
        scores = rq_col * (products[j] * rk_row) * decay
        dscore = dscores[j] * decay
        dp_ref[j] = dot_split(split(scores), owns[j], TN)
        dqs.append(dot_left(dscore * rk_row, kb[j]))
        hi, lo = split(dscore * rq_col)
        dk_ref[j] = dot(cat([hi, lo], 0), cat([qb[j], qb[j]], 0), TN)
    for j in group:
        dm = dm_ref[j]
        lefts = [split(dm * weights[:, (level + 1) * GROUP + j : (level + 1) * GROUP + j + 1]) for level in range(LEVELS)]
        rights = [split(bucket_of(x, j, level, near_refs, pair_refs, scratch_ref)) for level in range(LEVELS)]
        left = cat([p[0] for p in lefts], 1), cat([p[1] for p in lefts], 1)
        right = cat([p[0] for p in rights], 1), cat([p[1] for p in rights], 1)
        dqs[j] = dqs[j] + dot_split(left, right, NT)
    for j in group:
        qf = qb[j].astype(F32)
        along = jnp.sum(dqs[j] * qf, axis=1, keepdims=True)
        gq_ref[:, j * N : (j + 1) * N] = (rqs[j] * (dqs[j] - qf * (rqs[j] * rqs[j] * along))).astype(BF16)


def final_kernel(
    x_ref, key_ref, value_ref, cols_ref, rows_ref, norm_ref, coef_ref, inv_ref, pseudo_ref, dp_ref, dk_ref,
    p0_ref, p1_ref, n0_ref, n1_ref, a0_ref, a1_ref, a2_ref, a3_ref, gk_ref, gv_ref, gb_ref, scratch_ref, mask_ref,
):
    x = x_ref[0]
    group = range(GROUP)

    @pl.when(pl.program_id(0) == 0)
    def _():
        row, col = iotas()
        mask_ref[...] = jnp.where(row > col, 0.0, -1e30)

    for m, ref in enumerate((a0_ref, a1_ref, a2_ref, a3_ref)):
        scratch_ref[x ^ m] = ref[...]
    kb = [key_ref[:, j * N : (j + 1) * N] for j in group]
    gs, rk_cols, trailings, decays, pseudos = [], [], [], [], []
    for j in group:
        rows = slice((j >> 1) * HALF, (j >> 1) * HALF + HALF)
        parts = []
        for half in range(2):
            quarter = 2 * (j & 1) + half
            parts.append(
                coef_ref[0, 0, j : j + 1, :] * from_halves((p0_ref, p1_ref), (x ^ 3) ^ quarter, rows)
                + from_halves((n0_ref, n1_ref), (x ^ 1) ^ quarter, rows)
                + coef_ref[1, 0, j : j + 1, :] * scratch_ref[quarter, rows, :]
            )
        gs.append(split(cat(parts, 0)))
    ups = [dot(cat([kb[j], kb[j]], 1), cat([gs[j][0], gs[j][1]], 0), NN) for j in group]
    inners = [dot(k, k, NT) for k in kb]
    dps = []
    for j in group:
        rk_cols.append(inv_norm_col(kb[j].astype(F32)))
        cum_col = cols_ref[0, :, j : j + 1]
        cum_row = rows_ref[0, j : j + 1, :]
        trailings.append(jnp.exp(cum_row[:, N - 1 : N] - cum_col))
        decays.append(jnp.exp((cum_col - cum_row) + mask_ref[...]))
        dps.append(split(dp_ref[j] + (trailings[j] * rk_cols[j]) * ups[j]))
    dxs = [dot_split(split(inv_ref[j]), dps[j], TN) for j in group]
    pseudos = [split(pseudo_ref[j]) for j in group]
    dks = [dk_ref[j] + trailings[j] * dot_split(pseudos[j], gs[j], NT) for j in group]
    das = [dot_split(split(dxs[j]), pseudos[j], NT) for j in group]
    backs, fronts = [], []
    lane = lax.broadcasted_iota(jnp.int32, (N, 8), 1)
    grad_beta = jnp.zeros((N, 8), F32)
    for j in group:
        vf = value_ref[:, j * N : (j + 1) * N].astype(F32)
        rk_row = norm_ref[0, j : j + 1, :]
        beta_col = cols_ref[0, :, GROUP + j : GROUP + j + 1]
        gv_ref[:, j * N : (j + 1) * N] = (beta_col * dxs[j]).astype(BF16)
        da = das[j] * decays[j]
        along = jnp.sum(dxs[j] * vf - rk_cols[j] * (da * (rk_row * inners[j])), axis=1, keepdims=True)
        grad_beta = jnp.where(lane == j, along, grad_beta)
        da = da * beta_col
        fronts.append(dot_left(da * rk_row, kb[j]))
        hi, lo = split(da * rk_cols[j])
        backs.append(dot(cat([hi, lo], 0), cat([kb[j], kb[j]], 0), TN))
    gb_ref[0] = grad_beta.T
    for j in group:
        kf = kb[j].astype(F32)
        dk = dks[j] - fronts[j] - backs[j]
        along = jnp.sum(dk * kf, axis=1, keepdims=True)
        gk_ref[:, j * N : (j + 1) * N] = (rk_cols[j] * (dk - kf * (rk_cols[j] * rk_cols[j] * along))).astype(BF16)


def call(kernel, prefetch, ins, in_specs, outs, out_specs, scratch=()):
    heads = 16
    grid_spec = pltpu.PrefetchScalarGridSpec(
        num_scalar_prefetch=len(prefetch),
        grid=(heads // GROUP,),
        in_specs=in_specs,
        out_specs=out_specs,
        scratch_shapes=list(scratch),
    )
    return pl.pallas_call(
        kernel,
        grid_spec=grid_spec,
        out_shape=outs,
        interpret=INTERPRET,
        compiler_params=pltpu.CompilerParams(dimension_semantics=("arbitrary",)),
    )(*prefetch, *ins)


def spec(shape, index):
    return pl.BlockSpec(shape, lambda i, *_: index(i))


TOKENS = spec((N, GROUP * N), lambda i: (0, i))
COLS = spec((1, N, 8), lambda i: (i, 0, 0))
WEIGHTS = spec((1, 8 * GROUP, N), lambda i: (i, 0, 0))
ROWS = spec((1, 8, N), lambda i: (i, 0, 0))
NORMS = spec((1, GROUP, N), lambda i: (i, 0, 0))
SQUARE = spec((GROUP, N, N), lambda i: (i, 0, 0))
SLOTS = spec((4, N, N), lambda i: (0, i, 0))
PAIRS = spec((2, N, N), lambda i: (0, i, 0))
PIECE = spec((N, N), lambda i: (i, 0))


def shape(*dims, dtype=F32):
    return jax.ShapeDtypeStruct(dims, dtype)


def permute(value, flip, only=None):
    size = lax.axis_size("ctx")
    pairs = [(s, s ^ flip) for s in range(size) if only is None or (s & 3) in only]
    return lax.ppermute(value, "ctx", pairs)


def block(query, key, value, beta, log_gate, level_weight, norm_gain, grad_out, grad_final_state):
    heads = beta.shape[1]
    device = lax.axis_index("ctx")
    x = device & 3
    z = device >> 2
    xs = jnp.reshape(x, (1,)).astype(jnp.int32)

    square = shape(heads, N, N)
    whole = spec((heads, N), lambda i: (0, 0))
    r0, r1, r2, r3, s0, s1, pseudo, inverse, norms, cols, rows, own_total = call(
        solve_kernel, (xs,), (log_gate.T, beta.T, key, value),
        [whole, whole, TOKENS, TOKENS],
        [shape(4 * N + 16, N)] * 4 + [shape(2, 4 * N, N)] * 2
        + [square, square, shape(4, GROUP, N), shape(4, N, 8), shape(4, 8, N), shape(heads, N)],
        [spec((4 * N + 16, N), lambda i: (0, 0))] * 4 + [PAIRS] * 2 + [SQUARE, SQUARE, NORMS]
        + [spec((4, N, 8), lambda i: (0, 0, 0)), spec((4, 8, N), lambda i: (0, 0, 0)), whole],
        scratch=[pltpu.VMEM((6, N, N), F32), pltpu.VMEM((4, N, N), F32)],
    )

    def pick(tile):
        pairs = tile.reshape(8, 2, N)
        return jnp.where(x >= 2, pairs[:, 1], pairs[:, 0])[:, None, :]

    def quarter(rows_):
        return rows_[: 4 * N].reshape(8, HALF, N)

    gathered = [r0] + [permute(r, m) for m, r in ((1, r1), (2, r2), (3, r3))]
    totals = [own_total] + [g[4 * N :] for g in gathered[1:]]
    nears = [permute(s, 1, only=(0, 1, 2)) for s in (s0, s1)]
    after = []
    for m in range(4):
        after.append(sum(jnp.where((x ^ k) > (x ^ m), totals[k], 0.0) for k in range(4) if k != m))
    before = sum(jnp.where((x ^ k) < x, totals[k], 0.0) for k in range(1, 4))
    group_total = sum(totals)
    aggregate = sum(jnp.exp(pick(after[m])) * quarter(gathered[m]) for m in range(4))

    intra = call(
        intra_kernel, (), (query, key, cols, rows, norms, pseudo),
        [TOKENS, TOKENS, COLS, ROWS, NORMS, SQUARE], square, SQUARE,
    )

    omegas = [
        jnp.where(x & 1 == 1, jnp.ones((heads, N), F32), 0.0),
        jnp.where(x >= 2, jnp.exp(jnp.where(x & 1 == 1, totals[1], 0.0)), 0.0),
    ]
    records = []
    pieces = []
    offset = before
    pairs = []
    for degree, flip in enumerate((1, 2, 7)):
        upper = (z >> degree) & 1 == 1
        payload = cat([aggregate.reshape(4 * N, N), group_total], 0)
        received = permute(payload, flip << 2)
        if degree == 0:
            decays = totals[1].reshape(8, 2, N), own_total.reshape(8, 2, N)
            keep, take = (jnp.exp(d).transpose(1, 0, 2)[:, None, :, None, :] for d in decays)
            keep = jnp.where(x == 0, keep, 1.0)
            take = jnp.where(x == 0, 1.0, take)
            for k, own in enumerate((s0, s1)):
                other = nears[k].reshape(2, 8, HALF, N)[::-1]
                payload = keep[k] * own.reshape(2, 8, HALF, N) + take[k] * other
                pairs.append(permute(payload.reshape(2, 4 * N, N), 3, only=(0, 1)))
        partner_total = received[4 * N :]
        omegas.append(jnp.where(upper, jnp.exp(offset), 0.0))
        records.append((upper, group_total, partner_total))
        third = permute(received, 3)
        first = permute(received, 1)
        second = permute(received, 2) if degree > 0 else permute(third, 1)
        pieces += [received, first, second, third]
        aggregate = jnp.where(
            upper,
            jnp.exp(pick(group_total)) * quarter(received) + aggregate,
            jnp.exp(pick(partner_total)) * aggregate + quarter(received),
        )
        offset = jnp.where(upper, offset + partner_total, offset)
        group_total = group_total + partner_total
    final_state = lax.dynamic_index_in_dim(aggregate, z, 0, keepdims=False)
    growth = jnp.exp(rows[:, :GROUP].reshape(1, heads, N)) * jnp.stack(omegas)
    growth = cat([jnp.ones((1, heads, N), F32), growth], 0)
    weights = jnp.pad(level_weight.transpose(2, 1, 0) * growth, ((0, 2), (0, 0), (0, 0)))
    weights = weights.reshape(8, 4, GROUP, N).transpose(1, 0, 2, 3).reshape(4, 8 * GROUP, N)

    outs = call(
        cross_kernel, (xs,),
        (query, grad_out, intra, weights, norm_gain.reshape(1, N), *nears, *pairs, *pieces),
        [TOKENS, TOKENS, SQUARE, WEIGHTS, spec((1, N), lambda i: (0, 0))] + [PAIRS] * 4 + [PIECE] * 12,
        [shape(4, 4 * N, N)] + [shape(2, 4 * N, N)] * 6 + [shape(4 * N + 8, N)] * 4 + [square, shape(4, 8 * GROUP, N)],
        [SLOTS] + [PAIRS] * 6
        + [spec((4 * N + 8, N), lambda i: (0, 0))] * 4 + [SQUARE, WEIGHTS],
        scratch=[pltpu.VMEM((3, 4, N, N), F32), pltpu.VMEM((4, 4, N, N), F32), pltpu.VMEM((8, N), F32)],
    )
    grad_near, grad_pairs = outs[0], outs[1:3]
    grads34, grads5 = outs[3:7], outs[7:11]
    grad_mixture, grad_level_rows = outs[11:]

    top = grads5[0] + sum(permute(grads5[m], m) for m in range(1, 4))
    pair_backs = [permute(g, 3, only=(2, 3)) for g in grad_pairs]
    middle = []
    for level in range(2):
        kept, sent = grads34[2 * level : 2 * level + 2]
        first = permute(sent, 1)
        second = permute(kept[1] + first[1], 3)
        middle.append(kept[0] + first[0] + second)

    blocks = lax.broadcasted_iota(jnp.int32, (8, 1, 1), 0)
    adjoint = jnp.where(blocks == z, grad_final_state[None], 0.0)
    gain_rows = top[4 * N :]
    bucket_grads = [middle[0], middle[1], top[: 4 * N]]
    for degree, flip in ((2, 7), (1, 2), (0, 1)):
        upper, group_total, partner_total = records[degree]
        outgoing = quarter(bucket_grads[degree]) + jnp.where(upper, jnp.exp(pick(group_total)) * adjoint, adjoint)
        incoming = permute(cat([outgoing.reshape(4 * N, N), gain_rows], 0), flip << 2)
        adjoint = jnp.where(upper, adjoint, jnp.exp(pick(partner_total)) * adjoint) + quarter(incoming)
        gain_rows = gain_rows + incoming[4 * N :]
    adjoint = adjoint.reshape(4 * N, N)
    adjoints = [adjoint] + [permute(adjoint, m) for m in range(1, 4)]

    near_backs = []
    for k in range(2):
        back = pair_backs[1 - k].reshape(2, 8, HALF, N)[::-1]
        own = grad_near[2 * k : 2 * k + 2].reshape(2, 8, HALF, N)
        near_backs.append(permute((own + take[k] * back).reshape(2, 4 * N, N), 1, only=(0, 1, 3)))

    grad_query, grad_pseudo, grad_key_part = call(
        query_kernel, (xs,),
        (query, key, cols, rows, norms, weights, pseudo, grad_mixture, *nears, *pairs, *pieces),
        [TOKENS, TOKENS, COLS, ROWS, NORMS, WEIGHTS, SQUARE, SQUARE] + [PAIRS] * 4 + [PIECE] * 12,
        [shape(N, heads * N, dtype=BF16), square, square], [TOKENS, SQUARE, SQUARE],
        scratch=[pltpu.VMEM((3, 4, N, N), F32), pltpu.VMEM((N, N), F32)],
    )

    coef_pair = jnp.where(x < 2, jnp.exp(jnp.where(x == 0, totals[1], 0.0)), 0.0)
    coefs = jnp.stack([coef_pair, jnp.exp(after[0])]).reshape(2, 4, GROUP, N)
    grad_key, grad_value, grad_beta_rows = call(
        final_kernel, (xs,),
        (key, value, cols, rows, norms, coefs, inverse, pseudo, grad_pseudo, grad_key_part, *pair_backs, *near_backs, *adjoints),
        [TOKENS, TOKENS, COLS, ROWS, NORMS, spec((2, 1, GROUP, N), lambda i: (0, i, 0, 0))]
        + [SQUARE] * 4 + [PAIRS] * 4 + [PIECE] * 4,
        [shape(N, heads * N, dtype=BF16), shape(N, heads * N, dtype=BF16), shape(4, 8, N)],
        [TOKENS, TOKENS, ROWS],
        scratch=[pltpu.VMEM((4, N, N), F32), pltpu.VMEM((N, N), F32)],
    )
    return (
        grad_query,
        grad_key,
        grad_value,
        grad_beta_rows[:, :GROUP].reshape(heads, N).T,
        (grad_level_rows.reshape(4, 8, GROUP, N)[:, :6].transpose(1, 0, 2, 3).reshape(6, heads, N) * growth).transpose(2, 1, 0),
        gain_rows.sum(axis=0),
        final_state,
    )


def solution(mesh):
    tokens = P(("rep", "ctx"), None)
    levels = P(("rep", "ctx"), None, None)
    in_specs = (tokens, tokens, tokens, tokens, tokens, levels, P(), tokens, tokens)
    out_specs = (tokens, tokens, tokens, tokens, levels, P("rep"), tokens)
    return jax.shard_map(block, mesh=mesh, in_specs=in_specs, out_specs=out_specs, check_vma=False)
```

```python
import jax
import jax.numpy as jnp
from jax import lax
from jax.experimental import pallas as pl
from jax.experimental.pallas import tpu as pltpu
from jax.sharding import PartitionSpec as P


EPS = 1e-06
F32 = jnp.float32
BF16 = jnp.bfloat16
N = 128
HALF = 64
GROUP = 4
LEVELS = 5
INTERPRET = False


NN = ((1,), (0,))
NT = ((1,), (1,))
TN = ((0,), (0,))


def dot(a, b, dims):
    return lax.dot_general(a, b, (dims, ((), ())), preferred_element_type=F32)


def split(a):
    hi = a.astype(BF16)
    return hi, (a - hi.astype(F32)).astype(BF16)


def cat(parts, axis):
    return jnp.concatenate(parts, axis=axis)


def dot_left(a, b, dims=NN):
    hi, lo = split(a)
    ca, cb = dims[0][0], dims[1][0]
    return dot(cat([hi, lo], ca), cat([b, b], cb), dims)


def dot_split(a, b, dims=NN):
    ca, cb = dims[0][0], dims[1][0]
    return dot(cat([a[0], a[1], a[0]], ca), cat([b[0], b[0], b[1]], cb), dims)


def dot_full(a, b, dims=NN):
    return dot_split(split(a), split(b), dims)


def iotas():
    return (
        lax.broadcasted_iota(jnp.int32, (N, N), 0),
        lax.broadcasted_iota(jnp.int32, (N, N), 1),
    )


def inv_norm_col(raw):
    return lax.rsqrt(jnp.sum(raw * raw, axis=1, keepdims=True) + EPS)


def unit_lower_inverse(lowers, mask_ref):
    row16 = lax.broadcasted_iota(jnp.int32, (16, N), 0)
    col16 = lax.broadcasted_iota(jnp.int32, (16, N), 1)
    base = col16 & 112
    start = jnp.where((col16 & 15) == row16, 1.0, 0.0).astype(F32)
    packed = [(a * mask_ref[1]).reshape(8, 16, N).sum(axis=0) for a in lowers]
    inverses = [start for _ in lowers]
    for j in range(15):
        index = base | j
        for h, rows in enumerate(packed):
            column = jnp.take_along_axis(rows, index, axis=1, mode="promise_in_bounds")
            inverses[h] = inverses[h] - column * inverses[h][j : j + 1, :]
    inverses = [jnp.broadcast_to(a[None], (8, 16, N)).reshape(N, N) * mask_ref[1] for a in inverses]
    for level in range(3):
        pairs = [split(a) for a in inverses]
        inner = [dot_split(split(a * mask_ref[2 + level]), p) for a, p in zip(lowers, pairs)]
        inverses = [a - dot_split(p, split(c)) for a, p, c in zip(inverses, pairs, inner)]
    return inverses


def fill_masks(mask_ref):
    row, col = iotas()
    mask_ref[0] = jnp.where(row > col, 0.0, -1e30)
    mask_ref[1] = jnp.where((row >> 4) == (col >> 4), 1.0, 0.0)
    for level in range(3):
        bits = 4 + level
        below = ((row >> bits) & 1 == 1) & ((col >> bits) == (row >> bits) - 1)
        mask_ref[2 + level] = jnp.where(below, 1.0, 0.0)
    mask_ref[5] = jnp.where(row == col, 1.0, 0.0)


def token_sums(gate_ref, beta_ref, cols_ref, rows_ref, total_ref):
    row, col = iotas()
    gate = gate_ref[...]
    beta = beta_ref[...]
    upper = jnp.where(row <= col, 1.0, 0.0).astype(BF16)
    hi, lo = split(gate)
    rest = (gate - hi.astype(F32) - lo.astype(F32)).astype(BF16)
    cum = dot(cat([hi, lo, rest], 1), cat([upper] * 3, 0), NN)
    total_ref[...] = jnp.broadcast_to(cum[:, N - 1 : N], cum.shape)
    columns = cat([cum, beta], 0).T
    for s in range(4):
        part = slice(s * GROUP, (s + 1) * GROUP)
        rows_ref[s] = cat([cum[part], beta[part]], 0)
        cols_ref[s] = cat([columns[:, part], columns[:, 16 + s * GROUP : 16 + (s + 1) * GROUP]], 1)


def solve_kernel(
    x_ref, gate_ref, beta_ref, key_ref, value_ref,
    r0_ref, r1_ref, r2_ref, r3_ref, s0_ref, s1_ref,
    pseudo_ref, inv_ref, norm_ref, cols_ref, rows_ref, total_ref, mask_ref, gather_ref,
):
    ring_refs = r0_ref, r1_ref, r2_ref, r3_ref
    half_refs = s0_ref, s1_ref
    step = pl.program_id(0)
    x = x_ref[0]

    @pl.when(step == 0)
    def _():
        fill_masks(mask_ref)
        token_sums(gate_ref, beta_ref, cols_ref, rows_ref, total_ref)

    cols = cols_ref[step]
    rows = rows_ref[step]

    group = range(GROUP)
    kb = [key_ref[:, j * N : (j + 1) * N] for j in group]
    inner = [dot(k, k, NT) for k in kb]
    lowers, rk_cols = [], []
    for j in group:
        diagonal = inner[j] * mask_ref[5]
        rk_row = lax.rsqrt(jnp.sum(diagonal, axis=0, keepdims=True) + EPS)
        rk_cols.append(lax.rsqrt(jnp.sum(diagonal, axis=1, keepdims=True) + EPS))
        norm_ref[0, j : j + 1, :] = rk_row
        decay = jnp.exp((cols[:, j : j + 1] - rows[j : j + 1]) + mask_ref[0])
        lowers.append((cols[:, GROUP + j : GROUP + j + 1] * rk_cols[j]) * (decay * (rk_row * inner[j])))
    inverses = unit_lower_inverse(lowers, mask_ref)
    for j in group:
        inv_ref[j] = inverses[j]
    pseudos = [
        dot_left(inverses[j] * rows[GROUP + j : GROUP + j + 1], value_ref[:, j * N : (j + 1) * N])
        for j in group
    ]
    states = []
    for j in group:
        pseudo_ref[j] = pseudos[j]
        trailing = jnp.exp(rows[j : j + 1, N - 1 : N] - cols[:, j : j + 1]) * rk_cols[j]
        hi, lo = split(pseudos[j] * trailing)
        states.append(dot(cat([kb[j], kb[j]], 0), cat([hi, lo], 0), TN))
    for j in group:
        for half in range(2):
            rows = slice((j >> 1) * HALF, (j >> 1) * HALF + HALF)
            gather_ref[2 * (j & 1) + half, rows, :] = states[j][half * HALF : (half + 1) * HALF]
    base = pl.multiple_of(step * N, N)
    for slot in range(4):
        part = gather_ref[x ^ slot]
        ring_refs[slot][pl.ds(base, N), :] = part
        half_refs[slot >> 1][slot & 1] = part

    @pl.when(step == pl.num_programs(0) - 1)
    def _():
        for slot in range(4):
            ring_refs[slot][4 * N : 4 * N + 16, :] = total_ref[...]


def intra_kernel(query_ref, key_ref, cols_ref, rows_ref, norm_ref, pseudo_ref, intra_ref):
    row, col = iotas()
    group = range(GROUP)
    qb = [query_ref[:, j * N : (j + 1) * N] for j in group]
    products = [dot(qb[j], key_ref[:, j * N : (j + 1) * N], NT) for j in group]
    penalty = jnp.where(row >= col, 0.0, -1e30)
    scores = []
    for j in group:
        rq_col = inv_norm_col(qb[j].astype(F32))
        decay = jnp.exp((cols_ref[0, :, j : j + 1] - rows_ref[0, j : j + 1, :]) + penalty)
        scores.append(rq_col * (products[j] * norm_ref[0, j : j + 1, :]) * decay)
    for j in group:
        intra_ref[j] = dot_full(scores[j], pseudo_ref[j])


def place_pieces(x, pieces, scratch_ref):
    for level in range(len(pieces) // 4):
        for m in range(4):
            scratch_ref[level, x ^ m] = pieces[4 * level + m][...]


def from_halves(refs, slot, rows):
    return jnp.where(slot < 2, refs[0][slot & 1, rows, :], refs[1][slot & 1, rows, :])


def bucket_of(x, j, level, near_refs, pair_refs, scratch_ref):
    rows = slice((j >> 1) * HALF, (j >> 1) * HALF + HALF)
    parts = []
    for half in range(2):
        quarter = 2 * (j & 1) + half
        if level == 0:
            parts.append(from_halves(near_refs, (x ^ 1) ^ quarter, rows))
        elif level == 1:
            parts.append(from_halves(pair_refs, (x ^ 3) ^ quarter, rows))
        else:
            parts.append(scratch_ref[level - 2, quarter, rows, :])
    return cat(parts, 0)


def read_buckets(qb, buckets):
    pairs = [split(b) for b in buckets]
    return dot(cat([qb, qb], 1), cat([cat([p[0] for p in pairs], 1), cat([p[1] for p in pairs], 1)], 0), NN)


def bucket_grads(qb, weighted):
    pairs = [split(w) for w in weighted]
    return dot(cat([qb, qb], 0), cat([cat([p[0] for p in pairs], 1), cat([p[1] for p in pairs], 1)], 0), TN)


def scaled_columns(weights, rq_col, j, levels):
    scaled = weights * rq_col
    return [jnp.broadcast_to(scaled[:, l * GROUP + j : l * GROUP + j + 1], (N, N)) for l in levels]


def early_kernel(*refs):
    x_ref, query_ref, intra_ref, weight_ref = refs[:4]
    near_refs, pair_refs, pieces = refs[4:6], refs[6:8], refs[8:12]
    cross_ref, mix_ref, scratch_ref = refs[12:15]
    x = x_ref[0]
    group = range(GROUP)
    place_pieces(x, pieces, scratch_ref)
    weights = weight_ref[0].T
    qb = [query_ref[:, j * N : (j + 1) * N] for j in group]
    crosses = [
        read_buckets(qb[j], [bucket_of(x, j, level, near_refs, pair_refs, scratch_ref) for level in range(3)])
        for j in group
    ]
    for j in group:
        cross_ref[j] = crosses[j]
        columns = scaled_columns(weights, inv_norm_col(qb[j].astype(F32)), j, (1, 2, 3))
        mixture = weights[:, j : j + 1] * intra_ref[j]
        for level in range(3):
            mixture = mixture + columns[level] * crosses[j][:, level * N : (level + 1) * N]
        mix_ref[j] = mixture


def norm_kernel(*refs):
    x_ref, query_ref, out_ref, mix_ref, weight_ref, gain_ref = refs[:6]
    pieces = refs[6:14]
    cross_ref, dm_ref, g5_refs, g4_refs, g2_refs = refs[14], refs[15], refs[16:20], refs[20:22], refs[22:24]
    scratch_ref, gather_ref, gain_sum_ref = refs[24:27]
    step = pl.program_id(0)
    x = x_ref[0]
    group = range(GROUP)
    place_pieces(x, pieces, scratch_ref)
    gain = gain_ref[...]
    gain_sum = jnp.zeros((8, N), F32)
    weights = weight_ref[0].T
    qb = [query_ref[:, j * N : (j + 1) * N] for j in group]
    crosses = [
        read_buckets(qb[j], [bucket_of(x, j, level, (), (), scratch_ref) for level in (2, 3)]) for j in group
    ]
    weighted = []
    for j in group:
        cross_ref[j] = crosses[j]
        go = out_ref[:, j * N : (j + 1) * N].astype(F32)
        columns = scaled_columns(weights, inv_norm_col(qb[j].astype(F32)), j, (4, 5, 2))
        mixture = mix_ref[j] + columns[0] * crosses[j][:, :N] + columns[1] * crosses[j][:, N:]
        inverse_rms = lax.rsqrt(jnp.mean(mixture * mixture, axis=1, keepdims=True) + EPS)
        scaled = mixture * inverse_rms
        gain_sum = gain_sum + (go * scaled).reshape(N // 8, 8, N).sum(axis=0)
        dn = go * gain
        dm = inverse_rms * (dn - scaled * jnp.mean(dn * scaled, axis=1, keepdims=True))
        dm_ref[j] = dm
        weighted.append([dm * c for c in columns])
    for j in group:
        grads = bucket_grads(qb[j], weighted[j])
        rows = slice((j >> 1) * HALF, (j >> 1) * HALF + HALF)
        for half in range(2):
            for level in range(3):
                gather_ref[level, 2 * (j & 1) + half, rows, :] = grads[
                    half * HALF : (half + 1) * HALF, level * N : (level + 1) * N
                ]
    base = pl.multiple_of(step * N, N)
    for m in range(4):
        g4_refs[m in (1, 2)][m >> 1] = gather_ref[0, x ^ m]
        g5_refs[m][pl.ds(base, N), :] = gather_ref[1, x ^ m]
        g2_refs[m >> 1][m & 1] = gather_ref[2, x ^ m]

    @pl.when(step == 0)
    def _():
        gain_sum_ref[...] = jnp.zeros((8, N), F32)

    gain_sum_ref[...] += gain_sum

    @pl.when(step == pl.num_programs(0) - 1)
    def _():
        for m in range(4):
            g5_refs[m][4 * N : 4 * N + 8, :] = gain_sum_ref[...]


def late_kernel(*refs):
    x_ref, query_ref, intra_ref, weight_ref, early_ref, last_ref, dm_ref = refs[:7]
    g1_ref, g3_refs, level_ref, gather_ref = refs[7], refs[8:10], refs[10], refs[11]
    x = x_ref[0]
    group = range(GROUP)
    lane = lax.broadcasted_iota(jnp.int32, (N, 8 * GROUP), 1)
    weights = weight_ref[0].T
    levels = jnp.zeros((N, 8 * GROUP), F32)
    qb = [query_ref[:, j * N : (j + 1) * N] for j in group]
    weighted = []
    for j in group:
        dm = dm_ref[j]
        rq_col = inv_norm_col(qb[j].astype(F32))
        columns = scaled_columns(weights, rq_col, j, (1, 3))
        weighted.append([dm * c for c in columns])
        levels = jnp.where(lane == j, jnp.sum(dm * intra_ref[j], axis=1, keepdims=True), levels)
        for level in range(LEVELS):
            ref, at = (early_ref, level) if level < 3 else (last_ref, level - 3)
            along = jnp.sum(dm * ref[j, :, at * N : (at + 1) * N], axis=1, keepdims=True) * rq_col
            levels = jnp.where(lane == (level + 1) * GROUP + j, along, levels)
    level_ref[0] = levels.T
    for j in group:
        grads = bucket_grads(qb[j], weighted[j])
        rows = slice((j >> 1) * HALF, (j >> 1) * HALF + HALF)
        for half in range(2):
            quarter = 2 * (j & 1) + half
            part = grads[half * HALF : (half + 1) * HALF]
            g1_ref[x ^ quarter, rows, :] = part[:, 0:N]
            gather_ref[quarter, rows, :] = part[:, N : 2 * N]
    for m in range(4):
        g3_refs[m in (1, 2)][m >> 1] = gather_ref[x ^ m]


def query_kernel(*refs):
    x_ref, query_ref, key_ref, cols_ref, rows_ref, norm_ref, weight_ref, pseudo_ref, dm_ref = refs[:9]
    near_refs, pair_refs, pieces = refs[9:11], refs[11:13], refs[13:25]
    gq_ref, dp_ref, dk_ref, scratch_ref, mask_ref = refs[25:30]
    x = x_ref[0]
    group = range(GROUP)

    @pl.when(pl.program_id(0) == 0)
    def _():
        row, col = iotas()
        mask_ref[...] = jnp.where(row >= col, 0.0, -1e30)

    place_pieces(x, pieces, scratch_ref)
    qb = [query_ref[:, j * N : (j + 1) * N] for j in group]
    kb = [key_ref[:, j * N : (j + 1) * N] for j in group]
    products = [dot(q, k, NT) for q, k in zip(qb, kb)]
    weights = weight_ref[0].T
    owns = [split(dm_ref[j] * weights[:, j : j + 1]) for j in group]
    dscores = [dot_split(owns[j], split(pseudo_ref[j]), NT) for j in group]
    dqs, rqs = [], []
    for j in group:
        rq_col = inv_norm_col(qb[j].astype(F32))
        rqs.append(rq_col)
        rk_row = norm_ref[0, j : j + 1, :]
        decay = jnp.exp((cols_ref[0, :, j : j + 1] - rows_ref[0, j : j + 1, :]) + mask_ref[...])
        scores = rq_col * (products[j] * rk_row) * decay
        dscore = dscores[j] * decay
        dp_ref[j] = dot_split(split(scores), owns[j], TN)
        dqs.append(dot_left(dscore * rk_row, kb[j]))
        hi, lo = split(dscore * rq_col)
        dk_ref[j] = dot(cat([hi, lo], 0), cat([qb[j], qb[j]], 0), TN)
    for j in group:
        dm = dm_ref[j]
        lefts = [split(dm * weights[:, (level + 1) * GROUP + j : (level + 1) * GROUP + j + 1]) for level in range(LEVELS)]
        rights = [split(bucket_of(x, j, level, near_refs, pair_refs, scratch_ref)) for level in range(LEVELS)]
        left = cat([p[0] for p in lefts], 1), cat([p[1] for p in lefts], 1)
        right = cat([p[0] for p in rights], 1), cat([p[1] for p in rights], 1)
        dqs[j] = dqs[j] + dot_split(left, right, NT)
    for j in group:
        qf = qb[j].astype(F32)
        along = jnp.sum(dqs[j] * qf, axis=1, keepdims=True)
        gq_ref[:, j * N : (j + 1) * N] = (rqs[j] * (dqs[j] - qf * (rqs[j] * rqs[j] * along))).astype(BF16)


def final_kernel(
    x_ref, key_ref, value_ref, cols_ref, rows_ref, norm_ref, coef_ref, inv_ref, pseudo_ref, dp_ref, dk_ref,
    p0_ref, p1_ref, n0_ref, n1_ref, a0_ref, a1_ref, a2_ref, a3_ref, gk_ref, gv_ref, gb_ref, scratch_ref, mask_ref,
):
    x = x_ref[0]
    group = range(GROUP)

    @pl.when(pl.program_id(0) == 0)
    def _():
        row, col = iotas()
        mask_ref[...] = jnp.where(row > col, 0.0, -1e30)

    for m, ref in enumerate((a0_ref, a1_ref, a2_ref, a3_ref)):
        scratch_ref[x ^ m] = ref[...]
    kb = [key_ref[:, j * N : (j + 1) * N] for j in group]
    gs, rk_cols, trailings, decays, pseudos = [], [], [], [], []
    for j in group:
        rows = slice((j >> 1) * HALF, (j >> 1) * HALF + HALF)
        parts = []
        for half in range(2):
            quarter = 2 * (j & 1) + half
            parts.append(
                coef_ref[0, 0, j : j + 1, :] * from_halves((p0_ref, p1_ref), (x ^ 3) ^ quarter, rows)
                + from_halves((n0_ref, n1_ref), (x ^ 1) ^ quarter, rows)
                + coef_ref[1, 0, j : j + 1, :] * scratch_ref[quarter, rows, :]
            )
        gs.append(split(cat(parts, 0)))
    ups = [dot(cat([kb[j], kb[j]], 1), cat([gs[j][0], gs[j][1]], 0), NN) for j in group]
    inners = [dot(k, k, NT) for k in kb]
    dps = []
    for j in group:
        rk_cols.append(inv_norm_col(kb[j].astype(F32)))
        cum_col = cols_ref[0, :, j : j + 1]
        cum_row = rows_ref[0, j : j + 1, :]
        trailings.append(jnp.exp(cum_row[:, N - 1 : N] - cum_col))
        decays.append(jnp.exp((cum_col - cum_row) + mask_ref[...]))
        dps.append(split(dp_ref[j] + (trailings[j] * rk_cols[j]) * ups[j]))
    dxs = [dot_split(split(inv_ref[j]), dps[j], TN) for j in group]
    pseudos = [split(pseudo_ref[j]) for j in group]
    dks = [dk_ref[j] + trailings[j] * dot_split(pseudos[j], gs[j], NT) for j in group]
    das = [dot_split(split(dxs[j]), pseudos[j], NT) for j in group]
    backs, fronts = [], []
    lane = lax.broadcasted_iota(jnp.int32, (N, 8), 1)
    grad_beta = jnp.zeros((N, 8), F32)
    for j in group:
        vf = value_ref[:, j * N : (j + 1) * N].astype(F32)
        rk_row = norm_ref[0, j : j + 1, :]
        beta_col = cols_ref[0, :, GROUP + j : GROUP + j + 1]
        gv_ref[:, j * N : (j + 1) * N] = (beta_col * dxs[j]).astype(BF16)
        da = das[j] * decays[j]
        along = jnp.sum(dxs[j] * vf - rk_cols[j] * (da * (rk_row * inners[j])), axis=1, keepdims=True)
        grad_beta = jnp.where(lane == j, along, grad_beta)
        da = da * beta_col
        fronts.append(dot_left(da * rk_row, kb[j]))
        hi, lo = split(da * rk_cols[j])
        backs.append(dot(cat([hi, lo], 0), cat([kb[j], kb[j]], 0), TN))
    gb_ref[0] = grad_beta.T
    for j in group:
        kf = kb[j].astype(F32)
        dk = dks[j] - fronts[j] - backs[j]
        along = jnp.sum(dk * kf, axis=1, keepdims=True)
        gk_ref[:, j * N : (j + 1) * N] = (rk_cols[j] * (dk - kf * (rk_cols[j] * rk_cols[j] * along))).astype(BF16)


def call(kernel, prefetch, ins, in_specs, outs, out_specs, scratch=()):
    heads = 16
    grid_spec = pltpu.PrefetchScalarGridSpec(
        num_scalar_prefetch=len(prefetch),
        grid=(heads // GROUP,),
        in_specs=in_specs,
        out_specs=out_specs,
        scratch_shapes=list(scratch),
    )
    return pl.pallas_call(
        kernel,
        grid_spec=grid_spec,
        out_shape=outs,
        interpret=INTERPRET,
        compiler_params=pltpu.CompilerParams(dimension_semantics=("arbitrary",)),
    )(*prefetch, *ins)


def spec(shape, index):
    return pl.BlockSpec(shape, lambda i, *_: index(i))


TOKENS = spec((N, GROUP * N), lambda i: (0, i))
COLS = spec((1, N, 8), lambda i: (i, 0, 0))
WEIGHTS = spec((1, 8 * GROUP, N), lambda i: (i, 0, 0))
ROWS = spec((1, 8, N), lambda i: (i, 0, 0))
NORMS = spec((1, GROUP, N), lambda i: (i, 0, 0))
SQUARE = spec((GROUP, N, N), lambda i: (i, 0, 0))
SLOTS = spec((4, N, N), lambda i: (0, i, 0))
PAIRS = spec((2, N, N), lambda i: (0, i, 0))
PIECE = spec((N, N), lambda i: (i, 0))


def shape(*dims, dtype=F32):
    return jax.ShapeDtypeStruct(dims, dtype)


def permute(value, flip, only=None):
    size = lax.axis_size("ctx")
    pairs = [(s, s ^ flip) for s in range(size) if only is None or (s & 3) in only]
    return lax.ppermute(value, "ctx", pairs)


def block(query, key, value, beta, log_gate, level_weight, norm_gain, grad_out, grad_final_state):
    heads = beta.shape[1]
    device = lax.axis_index("ctx")
    x = device & 3
    z = device >> 2
    xs = jnp.reshape(x, (1,)).astype(jnp.int32)

    square = shape(heads, N, N)
    whole = spec((heads, N), lambda i: (0, 0))
    r0, r1, r2, r3, s0, s1, pseudo, inverse, norms, cols, rows, own_total = call(
        solve_kernel, (xs,), (log_gate.T, beta.T, key, value),
        [whole, whole, TOKENS, TOKENS],
        [shape(4 * N + 16, N)] * 4 + [shape(2, 4 * N, N)] * 2
        + [square, square, shape(4, GROUP, N), shape(4, N, 8), shape(4, 8, N), shape(heads, N)],
        [spec((4 * N + 16, N), lambda i: (0, 0))] * 4 + [PAIRS] * 2 + [SQUARE, SQUARE, NORMS]
        + [spec((4, N, 8), lambda i: (0, 0, 0)), spec((4, 8, N), lambda i: (0, 0, 0)), whole],
        scratch=[pltpu.VMEM((6, N, N), F32), pltpu.VMEM((4, N, N), F32)],
    )

    def pick(tile):
        pairs = tile.reshape(8, 2, N)
        return jnp.where(x >= 2, pairs[:, 1], pairs[:, 0])[:, None, :]

    def quarter(rows_):
        return rows_[: 4 * N].reshape(8, HALF, N)

    gathered = [r0] + [permute(r, m) for m, r in ((1, r1), (2, r2), (3, r3))]
    totals = [own_total] + [g[4 * N :] for g in gathered[1:]]
    nears = [permute(s, 1, only=(0, 1, 2)) for s in (s0, s1)]
    after = []
    for m in range(4):
        after.append(sum(jnp.where((x ^ k) > (x ^ m), totals[k], 0.0) for k in range(4) if k != m))
    before = sum(jnp.where((x ^ k) < x, totals[k], 0.0) for k in range(1, 4))
    group_total = sum(totals)
    aggregate = sum(jnp.exp(pick(after[m])) * quarter(gathered[m]) for m in range(4))

    intra = call(
        intra_kernel, (), (query, key, cols, rows, norms, pseudo),
        [TOKENS, TOKENS, COLS, ROWS, NORMS, SQUARE], square, SQUARE,
    )

    omegas = [
        jnp.where(x & 1 == 1, jnp.ones((heads, N), F32), 0.0),
        jnp.where(x >= 2, jnp.exp(jnp.where(x & 1 == 1, totals[1], 0.0)), 0.0),
    ]
    records = []
    pieces = []
    offset = before
    pairs = []
    for degree, flip in enumerate((1, 2, 7)):
        upper = (z >> degree) & 1 == 1
        payload = cat([aggregate.reshape(4 * N, N), group_total], 0)
        received = permute(payload, flip << 2)
        if degree == 0:
            decays = totals[1].reshape(8, 2, N), own_total.reshape(8, 2, N)
            keep, take = (jnp.exp(d).transpose(1, 0, 2)[:, None, :, None, :] for d in decays)
            keep = jnp.where(x == 0, keep, 1.0)
            take = jnp.where(x == 0, 1.0, take)
            for k, own in enumerate((s0, s1)):
                other = nears[k].reshape(2, 8, HALF, N)[::-1]
                payload = keep[k] * own.reshape(2, 8, HALF, N) + take[k] * other
                pairs.append(permute(payload.reshape(2, 4 * N, N), 3, only=(0, 1)))
        partner_total = received[4 * N :]
        omegas.append(jnp.where(upper, jnp.exp(offset), 0.0))
        records.append((upper, group_total, partner_total))
        third = permute(received, 3)
        first = permute(received, 1)
        second = permute(received, 2) if degree > 0 else permute(third, 1)
        pieces += [received, first, second, third]
        aggregate = jnp.where(
            upper,
            jnp.exp(pick(group_total)) * quarter(received) + aggregate,
            jnp.exp(pick(partner_total)) * aggregate + quarter(received),
        )
        offset = jnp.where(upper, offset + partner_total, offset)
        group_total = group_total + partner_total
    final_state = lax.dynamic_index_in_dim(aggregate, z, 0, keepdims=False)
    growth = jnp.exp(rows[:, :GROUP].reshape(1, heads, N)) * jnp.stack(omegas)
    growth = cat([jnp.ones((1, heads, N), F32), growth], 0)
    weights = jnp.pad(level_weight.transpose(2, 1, 0) * growth, ((0, 2), (0, 0), (0, 0)))
    weights = weights.reshape(8, 4, GROUP, N).transpose(1, 0, 2, 3).reshape(4, 8 * GROUP, N)

    crosses, mixed = call(
        early_kernel, (xs,), (query, intra, weights, *nears, *pairs, *pieces[:4]),
        [TOKENS, SQUARE, WEIGHTS] + [PAIRS] * 4 + [PIECE] * 4,
        [shape(heads, N, 3 * N), square], [spec((GROUP, N, 3 * N), lambda i: (i, 0, 0)), SQUARE],
        scratch=[pltpu.VMEM((1, 4, N, N), F32)],
    )
    last_crosses, grad_mixture, *outs = call(
        norm_kernel, (xs,), (query, grad_out, mixed, weights, norm_gain.reshape(1, N), *pieces[4:]),
        [TOKENS, TOKENS, SQUARE, WEIGHTS, spec((1, N), lambda i: (0, 0))] + [PIECE] * 8,
        [shape(heads, N, 2 * N), square] + [shape(4 * N + 8, N)] * 4 + [shape(2, 4 * N, N)] * 4,
        [spec((GROUP, N, 2 * N), lambda i: (i, 0, 0)), SQUARE] + [spec((4 * N + 8, N), lambda i: (0, 0))] * 4
        + [PAIRS] * 4,
        scratch=[pltpu.VMEM((2, 4, N, N), F32), pltpu.VMEM((3, 4, N, N), F32), pltpu.VMEM((8, N), F32)],
    )
    grads5, grads4, grad_pairs = outs[:4], outs[4:6], outs[6:]
    outs = call(
        late_kernel, (xs,), (query, intra, weights, crosses, last_crosses, grad_mixture),
        [TOKENS, SQUARE, WEIGHTS, spec((GROUP, N, 3 * N), lambda i: (i, 0, 0))]
        + [spec((GROUP, N, 2 * N), lambda i: (i, 0, 0)), SQUARE],
        [shape(4, 4 * N, N)] + [shape(2, 4 * N, N)] * 2 + [shape(4, 8 * GROUP, N)],
        [SLOTS] + [PAIRS] * 2 + [WEIGHTS],
        scratch=[pltpu.VMEM((4, N, N), F32)],
    )
    grad_near, grads3, grad_level_rows = outs[0], outs[1:3], outs[3]

    top = grads5[0] + sum(permute(grads5[m], m) for m in range(1, 4))
    pair_backs = [permute(g, 3, only=(2, 3)) for g in grad_pairs]
    middle = []
    for kept, sent in (grads3, grads4):
        first = permute(sent, 1)
        second = permute(kept[1] + first[1], 3)
        middle.append(kept[0] + first[0] + second)

    blocks = lax.broadcasted_iota(jnp.int32, (8, 1, 1), 0)
    adjoint = jnp.where(blocks == z, grad_final_state[None], 0.0)
    gain_rows = top[4 * N :]
    bucket_grads = [middle[0], middle[1], top[: 4 * N]]
    for degree, flip in ((2, 7), (1, 2), (0, 1)):
        upper, group_total, partner_total = records[degree]
        outgoing = quarter(bucket_grads[degree]) + jnp.where(upper, jnp.exp(pick(group_total)) * adjoint, adjoint)
        incoming = permute(cat([outgoing.reshape(4 * N, N), gain_rows], 0), flip << 2)
        adjoint = jnp.where(upper, adjoint, jnp.exp(pick(partner_total)) * adjoint) + quarter(incoming)
        gain_rows = gain_rows + incoming[4 * N :]
    adjoint = adjoint.reshape(4 * N, N)
    adjoints = [adjoint] + [permute(adjoint, m) for m in range(1, 4)]

    near_backs = []
    for k in range(2):
        back = pair_backs[1 - k].reshape(2, 8, HALF, N)[::-1]
        own = grad_near[2 * k : 2 * k + 2].reshape(2, 8, HALF, N)
        near_backs.append(permute((own + take[k] * back).reshape(2, 4 * N, N), 1, only=(0, 1, 3)))

    grad_query, grad_pseudo, grad_key_part = call(
        query_kernel, (xs,),
        (query, key, cols, rows, norms, weights, pseudo, grad_mixture, *nears, *pairs, *pieces),
        [TOKENS, TOKENS, COLS, ROWS, NORMS, WEIGHTS, SQUARE, SQUARE] + [PAIRS] * 4 + [PIECE] * 12,
        [shape(N, heads * N, dtype=BF16), square, square], [TOKENS, SQUARE, SQUARE],
        scratch=[pltpu.VMEM((3, 4, N, N), F32), pltpu.VMEM((N, N), F32)],
    )

    coef_pair = jnp.where(x < 2, jnp.exp(jnp.where(x == 0, totals[1], 0.0)), 0.0)
    coefs = jnp.stack([coef_pair, jnp.exp(after[0])]).reshape(2, 4, GROUP, N)
    grad_key, grad_value, grad_beta_rows = call(
        final_kernel, (xs,),
        (key, value, cols, rows, norms, coefs, inverse, pseudo, grad_pseudo, grad_key_part, *pair_backs, *near_backs, *adjoints),
        [TOKENS, TOKENS, COLS, ROWS, NORMS, spec((2, 1, GROUP, N), lambda i: (0, i, 0, 0))]
        + [SQUARE] * 4 + [PAIRS] * 4 + [PIECE] * 4,
        [shape(N, heads * N, dtype=BF16), shape(N, heads * N, dtype=BF16), shape(4, 8, N)],
        [TOKENS, TOKENS, ROWS],
        scratch=[pltpu.VMEM((4, N, N), F32), pltpu.VMEM((N, N), F32)],
    )
    return (
        grad_query,
        grad_key,
        grad_value,
        grad_beta_rows[:, :GROUP].reshape(heads, N).T,
        (grad_level_rows.reshape(4, 8, GROUP, N)[:, :6].transpose(1, 0, 2, 3).reshape(6, heads, N) * growth).transpose(2, 1, 0),
        gain_rows.sum(axis=0),
        final_state,
    )


def solution(mesh):
    tokens = P(("rep", "ctx"), None)
    levels = P(("rep", "ctx"), None, None)
    in_specs = (tokens, tokens, tokens, tokens, tokens, levels, P(), tokens, tokens)
    out_specs = (tokens, tokens, tokens, tokens, levels, P("rep"), tokens)
    return jax.shard_map(block, mesh=mesh, in_specs=in_specs, out_specs=out_specs, check_vma=False)
```
